32 devices in a mesh: dp: 4 (over y, core), mp: 8 (over z, x).
Axes of the slice: x: 2, y: 2, z: 4, core: 2. Of those that a mesh axis runs over, the one named last changes fastest.
Arguments:
- qkv: bfloat16 [4096, 3840], P(('dp', 'mp')), may hold values from -16 to 16
- send_pos: int32 [512], P(('dp', 'mp')), may hold values from 0 to 15, as said below
- recv_pos: int32 [512], P(('dp', 'mp')), may hold values from 0 to 15, as said below
- block_image: int32 [512], P(('dp', 'mp')), may hold values from 0 to 15, as said below
- owner: int32 [4096, 1], P(('dp', 'mp')), may hold values from 0 to 7; in each aligned block of 128 rows (0 to 127, 128 to 255, ...) at most 24 rows name the same one
- cotangent: bfloat16 [4096, 640], P(('dp', 'mp')), may hold values from -0.109375 to 0.109375
- out_weight: bfloat16 [1280, 1280], replicated, may hold values from -0.15625 to 0.15625
Outputs:
- attended_sent: bfloat16 [6144, 1280], P(('dp', 'mp'))
- grad_out_weight: float32 [409600], P(('dp', 'mp'))
The draws below stay inside these ranges and needn't reach their ends.
Inputs may be any that keep to these rules, and one draw needn't show every extreme that they name: `send_pos`: within a device the 16 values are distinct; value p * 4 + c sends the block to dp index p of the same mp index, slot c. Every device sends exactly 4 blocks to each of 4 distinct dp indices. `recv_pos`: within a device the 16 values are distinct; value q * 4 + c takes the block that dp index q of the same mp index sent in slot c to this device, and that block exists. Every device receives exactly 4 blocks from each of 4 distinct dp indices. `block_image`: never falls along a device's working blocks and starts at 0 on each device; an image is 1 to 16 blocks; some device holds one image of 16 blocks, and some device holds 16 images of one block each. Of one device's rows, at most 24 have the same owner, and some device has exactly 24 rows for some owner.
All inputs are finite; a program needn't handle non-finite values.
Results may differ from the reference program's by a relative error of at most 0.0057.
Values may be sent and summed in bfloat16 or wider, within the bound.
No kernel may reach another device: no remote copies, remote signals or barrier semaphores. Data moves between devices by JAX's collectives and lax.ppermute only.
A program may use at most 64 MiB of HBM per device.

```python
import math
import jax
import jax.numpy as jnp
import numpy as np
from jax import lax

D = 1280
HEADS = 16
HEAD_DIM = 80
GW = 640
BR = 8
NBW = 16
CAP = 4
ROWS = 128
MOST_R = 24
TOTAL_ROWS = 4096
N_DP = 4
N_MP = 8


def draw_qkv(key, part):
    shape = (TOTAL_ROWS, 3, HEADS, HEAD_DIM)
    base = jax.random.truncated_normal(jax.random.fold_in(key, 101), -4.0, 4.0, shape, jnp.float32)
    spread = jnp.exp(jax.random.uniform(jax.random.fold_in(key, 102), (TOTAL_ROWS, 1, HEADS, 1), jnp.float32, math.log(0.4), math.log(4.0)))
    is_query = jnp.arange(3)[None, :, None, None] == 0
    values = jnp.where(is_query, base * spread, base)
    return values.reshape(TOTAL_ROWS, 3 * D).astype(jnp.bfloat16)


def order_table(key):
    scores = jax.random.randint(key, (N_DP, N_MP, NBW), 0, 1 << 20) * NBW + jnp.arange(NBW, dtype=jnp.int32)
    return jnp.argsort(scores, axis=-1).astype(jnp.int32)


def plan_tables(key):
    groups = NBW // CAP
    base = jax.random.fold_in(key, 21)

    def column_shifts(index):
        return jax.random.permutation(jax.random.fold_in(base, index), N_DP)[:groups].astype(jnp.int32)
    shifts = jax.vmap(column_shifts)(jnp.arange(N_MP, dtype=jnp.int32))
    shift_grid = jnp.broadcast_to(shifts[None, :, :], (N_DP, N_MP, groups))
    dp_grid = jnp.arange(N_DP, dtype=jnp.int32)[:, None, None]
    send_edge = order_table(jax.random.fold_in(key, 22))
    send_shift = jnp.take_along_axis(shift_grid, send_edge // CAP, axis=2)
    send_table = (dp_grid + send_shift) % N_DP * CAP + send_edge % CAP
    recv_edge = order_table(jax.random.fold_in(key, 23))
    recv_shift = jnp.take_along_axis(shift_grid, recv_edge // CAP, axis=2)
    recv_table = (dp_grid - recv_shift) % N_DP * CAP + recv_edge % CAP
    return (send_table.reshape(-1).astype(jnp.int32), recv_table.reshape(-1).astype(jnp.int32))


def draw_send_pos(key, part):
    return plan_tables(key)[0]


def draw_recv_pos(key, part):
    return plan_tables(key)[1]


def draw_block_image(key, part):
    cuts = jax.random.randint(jax.random.fold_in(key, 31), (N_DP, N_MP, NBW), 0, 3) == 0
    first = jnp.arange(NBW)[None, None, :] == 0
    single = (jnp.arange(N_DP)[:, None, None] == 0) & (jnp.arange(N_MP)[None, :, None] == 0)
    every = (jnp.arange(N_DP)[:, None, None] == 1) & (jnp.arange(N_MP)[None, :, None] == 0)
    cuts = cuts | every
    cuts = cuts & jnp.logical_not(first) & jnp.logical_not(single)
    return jnp.cumsum(cuts.astype(jnp.int32), axis=-1).reshape(-1).astype(jnp.int32)


def level_of(rng, shape, cuts, least, largest):
    loudness, own = 1.0, jax.random.fold_in(rng, 6)
    for dim, blocks in cuts:
        draws = jnp.exp(jax.random.uniform(jax.random.fold_in(own, dim), (blocks,), jnp.float32, least / len(cuts), largest / len(cuts)))
        loudness = loudness * jnp.repeat(draws, shape[dim] // blocks).reshape([-1 if axis == dim else 1 for axis in range(len(shape))])
    return loudness


def assign_block(own_key, own, number, rows, count, top, bound, lean):
    ranking = jax.random.permutation(own_key, count)
    heavy_load, common = load_shares(count, rows * top, bound, lean, True), load_shares(count, rows * top, bound, lean, False)
    places = jnp.arange(count)

    def named(lengths, offset_by):
        used = int((lengths > 0).sum())
        fixed = max(1, used // 4)
        shifted = fixed + (places - fixed + offset_by * (used - fixed)) % max(1, count - fixed)
        return jnp.zeros((count,), jnp.int32).at[ranking[jnp.where(places < fixed, places, shifted)]].set(jnp.asarray(lengths, jnp.int32))

    lengths = jnp.where(number % 4 == 0, named(heavy_load, number // 4), named(common, number - number // 4 - 1))
    mixed = jax.random.permutation(jax.random.fold_in(own, 3), count)
    donor, taker = mixed[0:count // 2 * 2:2], mixed[1:count // 2 * 2:2]
    margin = jnp.minimum(lengths[donor] - 1, bound - lengths[taker]) // 2
    margin = jnp.where((donor == ranking[0]) | (taker == ranking[0]) | (lengths[taker] == 0), 0, jnp.maximum(margin, 0))
    shifted = jax.random.randint(jax.random.fold_in(own, 4), (count // 2,), 0, 1 << 20) % (margin + 1)
    lengths = lengths.at[donor].add(-shifted).at[taker].add(shifted)
    items = jnp.searchsorted(jnp.cumsum(lengths), jnp.arange(rows * top), side="right").astype(jnp.int32)
    table = items.reshape(top, rows).T
    table = table[jax.random.permutation(jax.random.fold_in(own, 1), rows)]
    offset_by = jax.random.randint(jax.random.fold_in(own, 2), (rows, 1), 0, top)
    return jnp.take_along_axis(table, (jnp.arange(top)[None, :] + offset_by) % top, axis=1)


def load_shares(amount, total, most, lean, full):
    portions = [(1 << 20) // math.isqrt(standing ** lean) + 1 for standing in range(1, amount + 1)]
    largest = most if full else min(most, max(-(-total // amount), total * portions[0] // sum(portions)))
    least = 1 if total - largest >= amount - 1 else 0
    given, spare = [largest] + [least] * (amount - 1), total - largest - least * (amount - 1)
    while spare > 0:
        free = [i for i in range(1, amount) if given[i] < largest] or [i for i in range(1, amount) if given[i] < most]
        mass, budget = sum([portions[i] for i in free]), spare
        for i in free:
            extra = min(most - given[i], max(1, budget * portions[i] // mass), spare)
            given[i] = given[i] + extra
            spare = spare - extra
    return np.array(given)


def bell_draw(stream_key, dims, deviation, bound, pieces=(), held_as=jnp.bfloat16):
    array = deviation * jax.random.normal(stream_key, dims, jnp.float32)
    if pieces:
        array = array * level_of(stream_key, dims, pieces, -0.22, 0.18)
    return jnp.clip(array, -bound, bound).astype(held_as)


def setup_inputs(seed: int = 0) -> dict:
    seeds = jax.random.split(jax.random.key(seed), 8)
    qkv = draw_qkv(jax.random.fold_in(seeds[7], 71), 0)
    send_pos = draw_send_pos(jax.random.fold_in(seeds[7], 71), 0)
    recv_pos = draw_recv_pos(jax.random.fold_in(seeds[7], 71), 0)
    block_image = draw_block_image(jax.random.fold_in(seeds[7], 71), 0)
    owner_keys = jax.random.split(jax.random.fold_in(seeds[4], 1), TOTAL_ROWS // ROWS)
    owner_turns = jax.random.permutation(jax.random.fold_in(seeds[4], 3), TOTAL_ROWS // ROWS)
    owner = jax.vmap(lambda own, number: assign_block(jax.random.fold_in(seeds[4], 2), own, number, ROWS, N_MP, 1, MOST_R, 1))(owner_keys, owner_turns).reshape((TOTAL_ROWS, 1))
    cotangent = bell_draw(seeds[5], (TOTAL_ROWS, GW), 0.007, 0.109375, ((0, 32),))
    out_weight = bell_draw(seeds[6], (D, D), D ** -0.5, 0.15625)
    return dict(qkv=qkv, send_pos=send_pos, recv_pos=recv_pos, block_image=block_image, owner=owner, cotangent=cotangent, out_weight=out_weight)


def attend(packed, images):
    count = packed.shape[0]
    whole = packed.astype(jnp.float32).reshape(count, 3, HEADS, HEAD_DIM)
    query = whole[:, 0]
    keys = whole[:, 1]
    values = whole[:, 2]
    scores = jnp.einsum('qhd,khd->hqk', query, keys) / math.sqrt(HEAD_DIM)
    row_image = jnp.repeat(images, BR)
    allowed = (row_image[:, None] == row_image[None, :])[None]
    masked = jnp.where(allowed, scores, -jnp.inf)
    highest = lax.optimization_barrier(jnp.max(masked, axis=-1, keepdims=True))
    weights = jnp.where(allowed, jnp.exp(masked - highest), 0.0)
    probs = (weights / lax.optimization_barrier(jnp.sum(weights, axis=-1, keepdims=True))).astype(jnp.bfloat16)
    context = jnp.einsum('hqk,khd->qhd', probs.astype(jnp.float32), values)
    return context.reshape(count, D).astype(jnp.bfloat16)

def attend_column(inputs):
    return jax.vmap(attend)(inputs[0], inputs[1])

def reference(qkv, send_pos, recv_pos, block_image, owner, cotangent, out_weight):
    width = 3 * D
    blocks = qkv.reshape(N_DP, N_MP, NBW, BR, width)
    sender = send_pos.reshape(N_DP, N_MP, NBW)
    taker = recv_pos.reshape(N_DP, N_MP, NBW)
    dp_grid = jnp.broadcast_to(jnp.arange(N_DP, dtype=jnp.int32)[:, None, None], (N_DP, N_MP, NBW))
    mp_grid = jnp.broadcast_to(jnp.arange(N_MP, dtype=jnp.int32)[None, :, None], (N_DP, N_MP, NBW))
    slot_grid = jnp.broadcast_to(jnp.arange(NBW, dtype=jnp.int32)[None, None, :], (N_DP, N_MP, NBW))
    table = jnp.zeros((N_DP, N_MP, N_DP * CAP), jnp.int32).at[dp_grid, mp_grid, sender].set(slot_grid)
    source_dp = (taker // CAP).astype(jnp.int32)
    source_slot = table[source_dp, mp_grid, (dp_grid * CAP + taker % CAP).astype(jnp.int32)]
    packed = blocks[source_dp, mp_grid, source_slot].reshape(N_DP, N_MP, ROWS, width)
    images = block_image.reshape(N_DP, N_MP, NBW)
    context = lax.map(attend_column, (packed, images))
    flat_context = context.reshape(TOTAL_ROWS, D)
    attended = jnp.dot(flat_context, out_weight, preferred_element_type=jnp.float32).astype(jnp.bfloat16)
    target = owner.reshape(N_DP, N_MP, ROWS)
    member = (target[..., None] == jnp.arange(N_MP, dtype=jnp.int32)).astype(jnp.int32)
    before = jnp.cumsum(member, axis=2) - member
    rank = lax.optimization_barrier(jnp.sum(before * member, axis=3)).astype(jnp.int32)
    row_dp = jnp.broadcast_to(jnp.arange(N_DP, dtype=jnp.int32)[:, None, None], (N_DP, N_MP, ROWS))
    row_mp = jnp.broadcast_to(jnp.arange(N_MP, dtype=jnp.int32)[None, :, None], (N_DP, N_MP, ROWS))
    sent = jnp.zeros((N_DP, N_MP, N_MP, MOST_R, D), jnp.bfloat16)
    sent = sent.at[row_dp, target, row_mp, rank].set(attended.reshape(N_DP, N_MP, ROWS, D))
    attended_sent = sent.reshape(N_DP * N_MP * N_MP * MOST_R, D)
    grad_matrix = jnp.dot(flat_context[:, :GW].T, cotangent, preferred_element_type=jnp.float32)
    return (attended_sent, grad_matrix.reshape(GW * GW))
```

```python
import functools
import math

import jax
import jax.numpy as jnp
from jax import lax
from jax.experimental import pallas as pl
from jax.experimental.pallas import tpu as pltpu
from jax.sharding import PartitionSpec as P

D = 1280
HEADS = 16
HEAD_DIM = 80
BR = 8
NBW = 16
CHUNKS = 2
LANES = 128
CORES = 2


ANY = pl.BlockSpec(memory_space=pl.ANY)
SMEM = pl.BlockSpec(memory_space=pltpu.SMEM)
VMEM = pl.BlockSpec(memory_space=pltpu.VMEM)
BF16 = jnp.bfloat16
F32 = jnp.float32


def shape(dims, dtype):
    return jax.ShapeDtypeStruct(dims, dtype)


def dot(a, b, dims=((1,), (0,))):
    return lax.dot_general(a, b, (dims, ((), ())), preferred_element_type=F32)


def cost(flops, moved):
    return pl.CostEstimate(flops=flops, bytes_accessed=moved, transcendentals=0)


def pack_kernel(n_dp, first, cols, send_ref, x_ref, *rest):
    outs, (slots, sem_in, sem_out) = rest[:n_dp], rest[n_dp:]
    me = lax.axis_index("dp")
    capacity = NBW // n_dp
    copies = []
    for block in range(NBW):
        slot = jnp.bitwise_xor(send_ref[block], me * capacity)
        for part in range(3):
            copy = pltpu.make_async_copy(
                x_ref.at[block, :, pl.ds(part * D + first, cols)],
                slots.at[slot, :, pl.ds(part * cols, cols)],
                sem_in.at[block * 3 + part],
            )
            copy.start()
            copies.append(copy)
    for copy in copies:
        copy.wait()
    copies = []
    for k in range(n_dp):
        copy = pltpu.make_async_copy(slots.at[pl.ds(k * capacity, capacity)], outs[k], sem_out.at[k])
        copy.start()
        copies.append(copy)
    for copy in copies:
        copy.wait()


def pack(chunk, n_dp, send_pos, blocks):
    cols = D // CHUNKS
    out = shape((NBW // n_dp, BR, 3 * cols), BF16)
    return pl.pallas_call(
        functools.partial(pack_kernel, n_dp, chunk * cols, cols),
        out_shape=(out,) * n_dp,
        in_specs=[SMEM, ANY],
        out_specs=(ANY,) * n_dp,
        scratch_shapes=[
            pltpu.VMEM((NBW, BR, 3 * cols), BF16),
            pltpu.SemaphoreType.DMA((NBW * 3,)),
            pltpu.SemaphoreType.DMA((n_dp,)),
        ],
        cost_estimate=cost(0, 4 * NBW * BR * 3 * cols),
        name=f"pack{chunk}",
    )(send_pos, blocks)


def attend_kernel(n_dp, n_mp, most, groups, first, chunk, recv_ref, image_ref, owner_ref, weight_ref, *rest):
    arrived, rest = rest[:n_dp], rest[n_dp:]
    last = chunk == CHUNKS - 1
    if chunk > 0:
        total_ref, rest = rest[0], rest[1:]
    out_ref, rest = rest[0], rest[1:]
    if chunk == 0:
        pieces, rest = rest[:groups], rest[groups:]
    packed, weight, bias, values, context, inverse, sem_in, sem_w, sem_out = rest[:9]
    me = lax.axis_index("dp")
    capacity = NBW // n_dp
    cols = D // CHUNKS
    count = NBW * BR
    for w in range(NBW):
        inverse[recv_ref[w]] = w
    copies = []
    for k in range(n_dp):
        for c in range(capacity):
            w = inverse[jnp.bitwise_xor(me, k) * capacity + c]
            copy = pltpu.make_async_copy(arrived[k].at[c], packed.at[w], sem_in.at[k * capacity + c])
            copy.start()
            copies.append(copy)
    fetch = pltpu.make_async_copy(weight_ref.at[pl.ds(chunk * cols, cols)], weight, sem_w.at[0])
    fetch.start()

    lanes = lax.broadcasted_iota(jnp.int32, (BR, count), 1)
    image = jnp.zeros((BR, count), jnp.int32)
    for w in range(NBW):
        image = jnp.where(lanes // BR == w, image_ref[w], image)
    for w in range(NBW):
        bias[pl.ds(w * BR, BR), :] = jnp.where(image == image_ref[w], 0.0, -1e30)

    owner = owner_ref[...]
    member = (lax.broadcasted_iota(jnp.int32, (n_mp, count), 0) == owner).astype(F32)
    earlier = lax.broadcasted_iota(jnp.int32, (count, count), 0) < lax.broadcasted_iota(
        jnp.int32, (count, count), 1
    )
    before = dot(member.astype(BF16), earlier.astype(F32).astype(BF16))
    rank = jnp.sum(before * member, axis=0, keepdims=True)
    position = owner.astype(F32) * most + rank
    rows = lax.broadcasted_iota(jnp.int32, (n_mp * most, count), 0).astype(F32)
    place = (rows == position).astype(F32).astype(BF16)

    for copy in copies:
        copy.wait()
    values[...] = packed[:, :, 2 * cols :].reshape(count, cols).T
    scale = math.log2(math.e) / math.sqrt(HEAD_DIM)
    for h in range(HEADS // CHUNKS):
        low, high = h * HEAD_DIM, (h + 1) * HEAD_DIM
        start, stop = low // LANES * LANES, -(-high // LANES) * LANES
        query = packed[:, :, start:stop].reshape(count, stop - start)
        keys = packed[:, :, cols + start : cols + stop].reshape(count, stop - start)
        lane = lax.broadcasted_iota(jnp.int32, query.shape, 1) + start
        query = jnp.where((lane >= low) & (lane < high), query, jnp.zeros_like(query))
        scores = dot(keys, query, ((1,), (1,))) + bias[...]
        highest = jnp.max(scores, axis=0, keepdims=True)
        weights = jnp.exp2((scores - highest) * scale)
        probs = (weights / jnp.sum(weights, axis=0, keepdims=True)).astype(BF16)
        context[pl.ds(low, HEAD_DIM), :] = dot(values[pl.ds(low, HEAD_DIM), :], probs).astype(BF16)

    if chunk == 0:
        group = lax.axis_index("mp") // (n_mp // groups)
        depth = cols // (n_dp * groups)
        sends = []
        for k in range(groups):
            for p in range(n_dp):
                begin = pl.multiple_of(p * (cols // n_dp) + jnp.bitwise_xor(group, k) * depth, BR)
                copy = pltpu.make_async_copy(
                    context.at[pl.ds(begin, depth), :],
                    pieces[k].at[pl.ds(p * depth, depth), :],
                    sem_out.at[k * n_dp + p],
                )
                copy.start()
                sends.append(copy)
    placed = dot(place, context[...], ((1,), (1,))).astype(BF16)
    fetch.wait()
    total = dot(placed, weight[...])
    if chunk > 0:
        total = total + total_ref[...]
    out_ref[...] = total.reshape(out_ref.shape).astype(out_ref.dtype)
    if chunk == 0:
        for copy in sends:
            copy.wait()


def attend(chunk, n_dp, n_mp, most, groups, recv_pos, block_image, owner, weight, arrived, total):
    cols = D // CHUNKS
    count = NBW * BR
    last = chunk == CHUNKS - 1
    outs = [shape((n_mp, most, D), BF16) if last else shape((n_mp * most, D), F32)]
    out_specs = [VMEM]
    if chunk == 0:
        outs += [shape((cols // groups, count), BF16)] * groups
        out_specs += [ANY] * groups
    carried = [] if total is None else [total]
    return pl.pallas_call(
        functools.partial(attend_kernel, n_dp, n_mp, most, groups, 0, chunk),
        out_shape=tuple(outs),
        in_specs=[SMEM, SMEM, VMEM, ANY] + [ANY] * n_dp + [VMEM] * len(carried),
        out_specs=tuple(out_specs),
        scratch_shapes=[
            pltpu.VMEM((NBW, BR, 3 * cols), BF16),
            pltpu.VMEM((cols, D), BF16),
            pltpu.VMEM((count, count), F32),
            pltpu.VMEM((cols, count), BF16),
            pltpu.VMEM((cols, count), BF16),
            pltpu.SMEM((NBW,), jnp.int32),
            pltpu.SemaphoreType.DMA((NBW,)),
            pltpu.SemaphoreType.DMA((1,)),
            pltpu.SemaphoreType.DMA((groups * n_dp,)),
        ],
        cost_estimate=cost(8 * count * count * D + 2 * n_mp * most * cols * D, 4 * cols * D + 6 * count * cols),
        name=f"attend{chunk}",
    )(recv_pos, block_image, owner, weight, *arrived, *carried)


def partial_kernel(groups, n_dp, *refs):
    pieces, cotangents, (keep_ref, send_ref, total) = refs[:groups], refs[groups : 2 * groups], refs[2 * groups :]
    total[...] = sum(dot(a[...], b[...]) for a, b in zip(pieces, cotangents)).reshape(total.shape)
    core = lax.rem(lax.axis_index("dp"), CORES)
    for y in range(n_dp // CORES):
        keep_ref[y] = total[y * CORES + core]
        send_ref[y] = total[y * CORES + 1 - core]


def partial_sums(groups, n_dp, pieces, cotangents):
    rows, window = pieces[0].shape[0], cotangents[0].shape[1]
    out = shape((n_dp // CORES, rows // n_dp, window), F32)
    return pl.pallas_call(
        functools.partial(partial_kernel, groups, n_dp),
        out_shape=(out, out),
        in_specs=[VMEM] * (2 * groups),
        out_specs=(VMEM, VMEM),
        scratch_shapes=[pltpu.VMEM((n_dp, rows // n_dp, window), F32)],
        cost_estimate=cost(2 * groups * rows * window * NBW * BR, 4 * rows * window * 3),
        name="partial",
    )(*pieces, *cotangents)


def split_kernel(across, share, keep_ref, got_ref, *rest):
    outs, total = rest[:-1], rest[-1]
    total[...] = keep_ref[...] + got_ref[...]
    y = lax.axis_index("dp") // CORES
    x = lax.rem(lax.axis_index("mp"), across)
    for k, out in enumerate(outs):
        slab = total[jnp.bitwise_xor(y, k // across)]
        column = jnp.bitwise_xor(x, k % across)
        piece = slab[:share]
        for c in range(1, across):
            piece = jnp.where(column == c, slab[c * share : (c + 1) * share], piece)
        out[...] = piece


def split_sums(across, share, keep, got):
    peers = keep.shape[0] * across
    out = shape((share, keep.shape[2]), F32)
    return pl.pallas_call(
        functools.partial(split_kernel, across, share),
        out_shape=(out,) * peers,
        in_specs=[VMEM, VMEM],
        out_specs=(VMEM,) * peers,
        scratch_shapes=[pltpu.VMEM(keep.shape, F32)],
        cost_estimate=cost(keep.size, 12 * keep.size),
        name="split",
    )(keep, got)


def finish_kernel(*refs):
    out = refs[-1]
    total = sum(ref[...] for ref in refs[:-1])
    pieces = total.shape[1] // LANES
    for c in range(pieces):
        out[pl.ds(c, total.shape[0], stride=pieces), :] = total[:, c * LANES : (c + 1) * LANES]


def finish(parts):
    rows, window = parts[0].shape
    return pl.pallas_call(
        finish_kernel,
        out_shape=shape((rows * window // LANES, LANES), F32),
        in_specs=[VMEM] * len(parts),
        out_specs=VMEM,
        cost_estimate=cost(4 * rows * window, 20 * rows * window),
        name="finish",
    )(*parts)


def exchange(arrays, axes, size, masks):
    return [arrays[0]] + [
        lax.ppermute(a, axes, [(s, s ^ mask) for s in range(size)]) for a, mask in zip(arrays[1:], masks[1:])
    ]


def across_of(n_mp):
    across = 1
    while across * across * 8 <= n_mp:
        across *= 2
    return across


def body(qkv, send_pos, recv_pos, block_image, owner, cotangent, out_weight):
    n_dp = lax.axis_size("dp")
    n_mp = lax.axis_size("mp")
    count, width = qkv.shape
    window = cotangent.shape[1]
    most = 3 * count // (2 * n_mp)
    across = across_of(n_mp)
    groups = n_mp // across
    share = window // (n_dp * n_mp)
    if window * CHUNKS != D:
        return plain_body(qkv, send_pos, recv_pos, block_image, owner, cotangent, out_weight)

    blocks = qkv.reshape(NBW, BR, width)
    sent = [pack(c, n_dp, send_pos, blocks) for c in range(CHUNKS)]
    arrived = [exchange(s, "dp", n_dp, range(n_dp)) for s in sent]
    z_masks = [k * across for k in range(groups)]
    cotangents = exchange([cotangent] * groups, "mp", n_mp, z_masks)

    owners = owner.reshape(1, count)
    total, *pieces = attend(
        0, n_dp, n_mp, most, groups, recv_pos, block_image, owners, out_weight, arrived[0], None
    )
    (outgoing,) = attend(
        1, n_dp, n_mp, most, groups, recv_pos, block_image, owners, out_weight, arrived[1], total
    )
    delivered = lax.all_to_all(outgoing, "mp", split_axis=0, concat_axis=0, tiled=True)

    pieces = exchange(pieces, "mp", n_mp, z_masks)
    keep, send = partial_sums(groups, n_dp, pieces, cotangents)
    got = lax.ppermute(send, "dp", [(s, s ^ 1) for s in range(n_dp)])
    parts = split_sums(across, share, keep, got)
    masks = [(k // across) * CORES * n_mp + k % across for k in range(len(parts))]
    parts = exchange(parts, ("dp", "mp"), n_dp * n_mp, masks)
    gradient = finish(parts)
    return (delivered.reshape(n_mp * most, D), gradient.reshape(share * window))


def plain_body(qkv, send_pos, recv_pos, block_image, owner, cotangent, out_weight):
    dp_count = lax.axis_size("dp")
    mp_count = lax.axis_size("mp")
    count, width = qkv.shape
    window = cotangent.shape[1]
    capacity = max(1, NBW // dp_count)
    positions = dp_count * capacity
    block_width = BR * width
    source_blocks = qkv.reshape(NBW, block_width)
    place = (send_pos[None, :] == jnp.arange(positions, dtype=jnp.int32)[:, None]).astype(BF16)
    outgoing = jnp.dot(place, source_blocks, preferred_element_type=F32).astype(BF16)
    incoming = lax.all_to_all(
        outgoing.reshape(dp_count, capacity * block_width), "dp", split_axis=0, concat_axis=0, tiled=True
    )
    select = (recv_pos[:, None] == jnp.arange(positions, dtype=jnp.int32)[None, :]).astype(BF16)
    packed = jnp.dot(select, incoming.reshape(positions, block_width), preferred_element_type=F32).astype(BF16)
    whole = packed.reshape(count, 3, HEADS, HEAD_DIM)
    query = whole[:, 0]
    keys = whole[:, 1]
    values = whole[:, 2]
    scores = jnp.einsum("qhd,khd->hqk", query, keys, preferred_element_type=F32) / math.sqrt(HEAD_DIM)
    row_image = jnp.repeat(block_image, BR)
    allowed = (row_image[:, None] == row_image[None, :])[None]
    masked = jnp.where(allowed, scores, -jnp.inf)
    highest = jnp.max(masked, axis=-1, keepdims=True)
    weights = jnp.where(allowed, jnp.exp(masked - highest), 0.0)
    probs = (weights / jnp.sum(weights, axis=-1, keepdims=True)).astype(BF16)
    context = jnp.einsum("hqk,khd->qhd", probs, values, preferred_element_type=F32)
    context = context.reshape(count, D).astype(BF16)
    attended = jnp.dot(context, out_weight, preferred_element_type=F32).astype(BF16)
    most_rows = 3 * count // (2 * mp_count)
    target = owner[:, 0]
    member = (target[:, None] == jnp.arange(mp_count, dtype=jnp.int32)[None, :]).astype(jnp.int32)
    before = jnp.cumsum(member, axis=0) - member
    rank = jnp.sum(before * member, axis=1)
    position = target * most_rows + rank
    place_rows = (
        position[None, :] == jnp.arange(mp_count * most_rows, dtype=jnp.int32)[:, None]
    ).astype(BF16)
    outgoing_rows = jnp.dot(place_rows, attended, preferred_element_type=F32).astype(BF16)
    delivered = lax.all_to_all(
        outgoing_rows.reshape(mp_count, most_rows * D), "mp", split_axis=0, concat_axis=0, tiled=True
    )
    delivered = delivered.reshape(mp_count * most_rows, D)
    context_part = context[:, :window]
    group_rows = lax.psum_scatter(
        jnp.einsum("rd,re->de", context_part, cotangent, preferred_element_type=F32),
        "dp",
        scatter_dimension=0,
        tiled=True,
    )
    gradient = lax.psum_scatter(group_rows.reshape(-1), "mp", scatter_dimension=0, tiled=True)
    return (delivered, gradient)


def splits_evenly(n_dp, n_mp):
    count, window = NBW * BR, D // CHUNKS
    groups = n_mp // across_of(n_mp)
    powers = all(n & (n - 1) == 0 for n in (n_dp, n_mp)) and n_dp >= CORES
    return (
        powers
        and NBW % n_dp == 0
        and 3 * count % (2 * n_mp * BR) == 0
        and window % (n_dp * n_mp) == 0
        and window % (n_dp * groups * BR) == 0
    )


def solution(mesh):
    placed = (
        P(("dp", "mp"), None),
        P(("dp", "mp")),
        P(("dp", "mp")),
        P(("dp", "mp")),
        P(("dp", "mp"), None),
        P(("dp", "mp"), None),
        P(),
    )
    even = splits_evenly(mesh.shape["dp"], mesh.shape["mp"])
    return jax.shard_map(
        body if even else plain_body,
        mesh=mesh,
        in_specs=placed,
        out_specs=(P(("dp", "mp"), None), P(("dp", "mp"))),
        check_vma=False,
    )
```
